32 devices in a mesh: clus: 4 (over y, x), trip: 4 (over z), mode: 2 (over core).
Axes of the slice: x: 2, y: 2, z: 4, core: 2. Of those that a mesh axis runs over, the one named last changes fastest.
Arguments:
- force_third: bfloat16 [8, 90, 8100], P('clus', 'mode'), may hold values from -0.0234375 to 0.0234375
- phase_angle: bfloat16 [8, 16], P('clus', 'trip'), may hold values from -3.140625 to 3.140625
- eigenvectors: bfloat16 [32, 90, 180], P('trip'), may hold values from -0.4375 to 0.4375
- frequencies: bfloat16 [32, 90], P('trip'), may hold values from 0.5 to 2
- deviation: bfloat16 [32, 90], P('trip'), may hold values from 0.5 to 2
- send_rows: int32 [4, 32], P('trip'), may hold values from 0 to 7
- trip_table: int32 [16, 3], P('trip'), may hold values from 0 to 31
- irreducible: int32 [16], P('trip'), may hold values from 0 to 3
- multiplicity: int32 [16], P('trip'), may hold values from 1 to 8
- drive_term: float32 [4, 90], P('trip', 'mode'), may hold values from -120 to 120
- boundary: float32 [4, 90], P('trip', 'mode'), may hold values from 5 to 40
Outputs:
- gamma_total: float32 [4, 90], P('trip', 'mode')
- new_deviation: float32 [4, 90], P('trip', 'mode')
The draws below stay inside these ranges and needn't reach their ends.
All inputs are finite; a program needn't handle non-finite values.
Results may differ from the reference program's by a relative error of at most 0.00095.
Values may be sent and summed in bfloat16 or wider, within the bound.
A program may use at most 64 MiB of HBM per device.

```python
import math
import jax
import jax.numpy as jnp
from jax import lax

M = 90
CL_DEV = 2
G_DEV = 8
RECV = 32
NR = 8
TT = 4
TRIPLETS = 16
NG = 32
NQ = 4
SLOT = 8
N_CLUS = 4
N_TRIP = 4


def with_ends(values, rng, smallest, top_value):
    dims = values.shape
    index_at = [jax.random.randint(jax.random.fold_in(rng, axis), (), 0, dims[axis]) for axis in range(len(dims))]
    values = values.at[tuple(index_at)].set(smallest)
    longest = dims.index(max(dims))
    index_at[longest] = (index_at[longest] + 1) % dims[longest]
    return values.at[tuple(index_at)].set(top_value)


def levels(own_key, extent, pieces, least, largest):
    def one(position, blocks):
        draws = jax.random.uniform(jax.random.fold_in(jax.random.fold_in(own_key, 6), position), (blocks,), jnp.float32, least / len(pieces), largest / len(pieces))
        return jnp.repeat(jnp.exp(draws), extent[position] // blocks).reshape((-1,) + (1,) * (len(extent) - position - 1))

    factor_of = one(*pieces[0])
    for cut in pieces[1:]:
        factor_of = factor_of * one(*cut)
    return factor_of


def bell_draw(key, extent, scale, bound, cuts=(), kind=jnp.bfloat16):
    result = jax.random.normal(key, extent, jnp.float32) * scale
    if len(cuts) > 0:
        result = levels(key, extent, cuts, -0.22, 0.18) * result
    return jnp.clip(result, min=-bound, max=bound).astype(kind)


def setup_inputs(seed: int = 0) -> dict:
    seeds = jax.random.split(jax.random.key(seed), 12)
    force_third = bell_draw(seeds[0], (NR, M, M * M), (M * M * NR) ** -0.5, 0.0234375, ((0, 4), (1, 2)))
    phase_angle = jnp.clip(jax.random.uniform(seeds[1], (NR, TRIPLETS), jnp.float32, -3.140625, 3.140625), -3.140625, 3.140625).astype(jnp.bfloat16)
    eigenvectors = bell_draw(seeds[2], (NG, M, 2 * M), (2 * M) ** -0.5, 0.4375, ((0, 4),))
    frequencies = jnp.clip(jnp.exp(math.log(2.0) - 1.3862944 * jax.random.uniform(seeds[3], (NG, M), jnp.float32) ** levels(seeds[3], (NG, M), ((0, 4),), -0.2, 0.2)), 0.5, 2.0).astype(jnp.bfloat16)
    deviation = jnp.clip(0.5 + 1.5 * jax.random.uniform(seeds[4], (NG, M), jnp.float32) ** levels(seeds[4], (NG, M), ((0, 4),), -0.2, 0.2), 0.5, 2.0).astype(jnp.bfloat16)
    send_rows = with_ends(jax.random.randint(seeds[5], (N_TRIP, RECV), 0, G_DEV), jax.random.fold_in(seeds[5], 1), 0, G_DEV - 1).astype(jnp.int32)
    trip_table = with_ends(jax.random.randint(seeds[6], (TRIPLETS, 3), 0, RECV), jax.random.fold_in(seeds[6], 1), 0, RECV - 1).astype(jnp.int32)
    irreducible = with_ends(jax.random.randint(seeds[7], (TRIPLETS,), 0, NQ), jax.random.fold_in(seeds[7], 1), 0, NQ - 1).astype(jnp.int32)
    multiplicity = with_ends(jax.random.randint(seeds[8], (TRIPLETS,), 1, 9), jax.random.fold_in(seeds[8], 1), 1, 8).astype(jnp.int32)
    drive_term = bell_draw(seeds[9], (NQ, M), 20.0, 120.0, ((0, 4), (1, 2)), jnp.float32)
    boundary = jnp.clip(jnp.exp(math.log(40.0) - 2.0794415 * jax.random.uniform(seeds[10], (NQ, M), jnp.float32) ** levels(seeds[10], (NQ, M), ((0, 4), (1, 2)), -0.2, 0.2)), 5.0, 40.0)
    return dict(force_third=force_third, phase_angle=phase_angle, eigenvectors=eigenvectors, frequencies=frequencies, deviation=deviation, send_rows=send_rows, trip_table=trip_table, irreducible=irreducible, multiplicity=multiplicity, drive_term=drive_term, boundary=boundary)


smearing = 0.3
highest = lax.Precision.HIGHEST


def rounded(values):
    return lax.optimization_barrier(values.astype(jnp.bfloat16)).astype(jnp.float32)


def gaussian_weights(freq_zero, freq_one, freq_two):
    decays = freq_zero - freq_one - freq_two
    merges = freq_zero + freq_one - freq_two
    scaled = 0.5 / (smearing * smearing)
    return (jnp.exp(-scaled * decays * decays) + jnp.exp(-scaled * merges * merges)) / (freq_zero * freq_one * freq_two)


def combine(by_real, by_imag, mode_count):
    return jnp.concatenate([by_real[..., :mode_count] - by_imag[..., mode_count:], by_real[..., mode_count:] + by_imag[..., :mode_count]], axis=-1)


def interaction(transform, vectors):
    mode_count = vectors.shape[1]
    real_part = transform[0].reshape(-1, mode_count)
    imag_part = transform[1].reshape(-1, mode_count)
    last_vec = vectors[2]
    flipped = jnp.concatenate([-last_vec[:, mode_count:], last_vec[:, :mode_count]], axis=1)
    section_one = jnp.dot(real_part, last_vec, precision=highest) + jnp.dot(imag_part, flipped, precision=highest)
    section_one = rounded(section_one).reshape(mode_count, mode_count, 2 * mode_count)
    middle = vectors[1]
    section_two = rounded(combine(jnp.einsum("abk,bj->ajk", section_one, middle[:, :mode_count], precision=highest), jnp.einsum("abk,bj->ajk", section_one, middle[:, mode_count:], precision=highest), mode_count))
    leading = vectors[0]
    return combine(jnp.einsum("as,ajk->sjk", leading[:, :mode_count], section_two, precision=highest), jnp.einsum("as,ajk->sjk", leading[:, mode_count:], section_two, precision=highest), mode_count)


def reference(force_third, phase_angle, eigenvectors, frequencies, deviation, send_rows, trip_table, irreducible, multiplicity, drive_term, boundary):
    clusters = force_third.astype(jnp.float32).reshape(N_CLUS, CL_DEV, M * M * M)
    triplets = jnp.arange(TRIPLETS, dtype=jnp.int32)
    owners = triplets // TT
    sources = trip_table // SLOT
    within = trip_table % SLOT
    grid_points = sources * G_DEV + send_rows[sources, owners[:, None] * SLOT + within]
    vectors_all = eigenvectors.astype(jnp.float32)
    freq_all = frequencies.astype(jnp.float32)
    occupied_all = deviation.astype(jnp.float32)

    def one_triplet(triplet):
        angles = phase_angle[:, triplet].astype(jnp.float32).reshape(N_CLUS, CL_DEV)
        cosines = rounded(jnp.cos(angles))
        sines = rounded(jnp.sin(angles))
        real_sum = rounded(jnp.sum(rounded(jnp.einsum("gr,grx->gx", cosines, clusters, precision=highest)), axis=0))
        imag_sum = rounded(jnp.sum(rounded(jnp.einsum("gr,grx->gx", sines, clusters, precision=highest)), axis=0))
        transform = jnp.stack([real_sum, imag_sum]).reshape(2, M, M * M)
        members = grid_points[triplet]
        amplitude = interaction(transform, vectors_all[members])
        squared = amplitude[..., :M] ** 2 + amplitude[..., M:] ** 2
        rates = freq_all[members]
        weights = squared * gaussian_weights(rates[0][:, None, None], rates[1][None, :, None], rates[2][None, None, :]) * multiplicity[triplet].astype(jnp.float32)
        occupied = occupied_all[members]
        totals = jnp.sum(weights, axis=(1, 2))
        couples = jnp.einsum("sjk,j->s", weights, occupied[1], precision=highest) + jnp.einsum("sjk,k->s", weights, occupied[2], precision=highest)
        return totals, couples

    totals, couples = lax.map(one_triplet, triplets)
    onehot = (irreducible[:, None] == jnp.arange(NQ, dtype=jnp.int32)[None, :]).astype(jnp.float32)
    rate = jnp.dot(onehot.T, totals, precision=highest)
    coupled = jnp.dot(onehot.T, couples, precision=highest)
    gamma_total = rate + boundary
    return gamma_total, (drive_term + coupled) / gamma_total
```

```python
import functools

import jax
import jax.numpy as jnp
from jax import lax
from jax.experimental import pallas as pl
from jax.experimental.pallas import tpu as pltpu
from jax.sharding import PartitionSpec as P

smearing = 0.3
MESH = pl.DeviceIdType.MESH
LANES = 128
f32 = jnp.float32
bf16 = jnp.bfloat16


def up(value, step):
    return -(-value // step) * step


def pick(index, options):
    chosen = options[0]
    for position in range(1, len(options)):
        chosen = jnp.where(index == position, options[position], chosen)
    return chosen


def kernel(
    dims,
    force_ref,
    eig_ref,
    send_rows_ref,
    table_ref,
    irr_ref,
    mult_ref,
    drive_ref,
    bound_ref,
    gamma_ref,
    dev_ref,
    blocks,
    outgoing,
    arrived,
    mine,
    other,
    zbuf,
    tre,
    tim,
    w0buf,
    ratebuf,
    coupbuf,
    msg,
    inbox,
    f_send,
    f_recv,
    e_send,
    e_recv,
    p_send,
    p_recv,
    m_send,
    m_recv,
):
    n_clus, n_trip, n_mode, modes, half, rp, cl, slot, chunk = dims
    ep = eig_ref.shape[1]
    npad = force_ref.shape[1]
    me_c = lax.axis_index("clus")
    me_t = lax.axis_index("trip")
    me_m = lax.axis_index("mode")
    sib = (me_c, me_t, 1 - me_m)

    peers = []
    for dt in range(n_trip):
        for dc in range(n_clus):
            if dt or dc:
                peers.append((dt, dc))

    def peer_id(dt, dc):
        return (lax.rem(me_c + dc, n_clus), lax.rem(me_t + dt, n_trip), me_m)

    barrier = pltpu.get_barrier_semaphore()
    for dt, dc in peers:
        pl.semaphore_signal(barrier, inc=1, device_id=peer_id(dt, dc), device_id_type=MESH)
    pl.semaphore_signal(barrier, inc=1, device_id=sib, device_id_type=MESH)

    for dt in range(n_trip):
        target = lax.rem(me_t + dt, n_trip)
        for j in range(slot):
            row = send_rows_ref[0, target * slot + j]
            outgoing[dt, j] = eig_ref[row]

    pl.semaphore_wait(barrier, len(peers) + 1)

    def xor_id(k):
        low, high = lax.rem(me_c, 2), me_c // 2
        if k & 1:
            low = 1 - low
        if k & 2:
            high = 1 - high
        return (high * 2 + low, me_t, me_m)

    def unit(k, m, r):
        return blocks.at[k, m, pl.ds(r * rp, rp)]

    started = []

    def send(src, dst, k, m, r, device):
        copy = pltpu.make_async_remote_copy(
            src_ref=src,
            dst_ref=dst,
            send_sem=f_send.at[k, m, r],
            recv_sem=f_recv.at[k, m, r],
            device_id=device,
            device_id_type=MESH,
        )
        copy.start()
        started.append(copy)

    def got(k, m, r):
        pltpu.make_async_remote_copy(
            src_ref=unit(k, m, r),
            dst_ref=unit(k, m, r),
            send_sem=f_send.at[k, m, r],
            recv_sem=f_recv.at[k, m, r],
            device_id=sib,
            device_id_type=MESH,
        ).wait_recv()

    def own(r):
        return force_ref.at[pl.ds(r * rp, rp)]

    send(own(0), unit(1, 0, 0), 1, 0, 0, xor_id(1))
    send(own(1), unit(2, 0, 1), 2, 0, 1, xor_id(2))
    send(own(1), unit(1, 0, 1), 1, 0, 1, xor_id(1))
    send(own(0), unit(2, 0, 0), 2, 0, 0, xor_id(2))
    for r in range(cl):
        send(own(r), unit(0, 1, r), 0, 1, r, sib)

    eig_copies = []
    for dt in range(1, n_trip):
        copy = pltpu.make_async_remote_copy(
            src_ref=outgoing.at[dt],
            dst_ref=arrived.at[dt],
            send_sem=e_send.at[dt],
            recv_sem=e_recv.at[dt],
            device_id=(me_c, lax.rem(me_t + dt, n_trip), me_m),
            device_id_type=MESH,
        )
        copy.start()
        eig_copies.append(copy)
    arrived[0] = outgoing[0]

    got(1, 0, 0)
    send(unit(1, 0, 0), unit(3, 0, 0), 3, 0, 0, xor_id(2))
    send(unit(1, 0, 0), unit(1, 1, 0), 1, 1, 0, sib)
    got(2, 0, 1)
    send(unit(2, 0, 1), unit(3, 0, 1), 3, 0, 1, xor_id(1))
    send(unit(2, 0, 1), unit(2, 1, 1), 2, 1, 1, sib)

    for copy in eig_copies:
        copy.wait()
    for j in range(3):
        entry = table_ref[me_c, j]
        source = entry // slot
        within = entry - source * slot
        offset = lax.rem(me_t - source + n_trip, n_trip)
        mine[j] = arrived[offset * 1, within]
    pair = pltpu.make_async_remote_copy(
        src_ref=mine,
        dst_ref=other,
        send_sem=p_send,
        recv_sem=p_recv,
        device_id=sib,
        device_id_type=MESH,
    )
    pair.start()
    pair.wait()

    first = me_m == 0

    def complex_of(j):
        a = mine[j].astype(f32)
        b = other[j].astype(f32)
        return jnp.where(first, a, b), jnp.where(first, b, a)

    re0, im0 = complex_of(0)
    re1, im1 = complex_of(1)
    re2, im2 = complex_of(2)
    f0 = re0[modes : modes + 1]
    f1, d1 = re1[modes : modes + 1], im1[modes : modes + 1]
    f2, d2 = re2[modes : modes + 1], im2[modes : modes + 1]

    def half_rows(mat):
        return pick(me_m, [mat[m * half : m * half + rp] for m in range(n_mode)])

    fill = jnp.zeros((rp - half, LANES), f32)

    def lead(mat, m):
        part = mat[m * half : (m + 1) * half]
        stacked = jnp.concatenate([part, fill] * cl, axis=0)
        return half_rows(jnp.transpose(stacked))

    lead_re = [lead(re0, m) for m in range(n_mode)]
    lead_im = [lead(im0, m) for m in range(n_mode)]
    lane_k = lax.broadcasted_iota(jnp.int32, (rp, cl * rp), 1)
    lane = lax.broadcasted_iota(jnp.int32, (1, LANES), 1)

    def weights(block_ref, m_rel):
        cosines, sines = [], []
        for r in range(cl):
            tail = block_ref[pl.ds(r * rp + rp - 16, 16), pl.ds(0, LANES)].astype(f32)
            at = 16 - (rp - half)
            cosines.append(jnp.sum(jnp.where(lane == me_c, tail[at : at + 1], 0.0), axis=1, keepdims=True))
            sines.append(jnp.sum(jnp.where(lane == me_c, tail[at + 1 : at + 2], 0.0), axis=1, keepdims=True))
        cosv, sinv = cosines[0], sines[0]
        for r in range(1, cl):
            cosv = jnp.where(lane_k >= r * rp, cosines[r], cosv)
            sinv = jnp.where(lane_k >= r * rp, sines[r], sinv)
        if m_rel == 0:
            wre = jnp.where(first, lead_re[0], lead_re[1])
            wim = jnp.where(first, lead_im[0], lead_im[1])
        else:
            wre = jnp.where(first, lead_re[1], lead_re[0])
            wim = jnp.where(first, lead_im[1], lead_im[0])
        return jnp.concatenate(
            [cosv * wre - sinv * wim, cosv * wim + sinv * wre], axis=0
        ).astype(bf16)

    def accumulate(refs, fresh):
        mats = [weights(ref, m_rel) for ref, m_rel in refs]

        def step(n, carry):
            cols = pl.ds(pl.multiple_of(n * chunk, chunk), chunk)
            total = None
            for mat, (ref, _) in zip(mats, refs):
                part = jnp.dot(mat, ref[:, cols], preferred_element_type=f32)
                total = part if total is None else total + part
            if not fresh:
                total = total + zbuf[:, cols]
            zbuf[:, cols] = total
            return carry

        lax.fori_loop(0, npad // chunk, step, 0)

    e2a = jnp.concatenate([re2, im2], axis=1)[:modes].astype(bf16)
    e2b = jnp.concatenate([-im2, re2], axis=1)[:modes].astype(bf16)
    row_id = lax.broadcasted_iota(jnp.int32, (ep, LANES), 0)
    e1re_t = jnp.transpose(jnp.where(row_id < modes, re1, 0.0))[:ep]
    e1im_t = jnp.transpose(jnp.where(row_id < modes, im1, 0.0))[:ep]
    left_a = jnp.concatenate([e1re_t, e1im_t], axis=0).astype(bf16)
    left_b = jnp.concatenate([-e1im_t, e1re_t], axis=0).astype(bf16)

    def column(row):
        return jnp.transpose(jnp.broadcast_to(row, (LANES, LANES)))

    w0buf[...] = half_rows(jnp.where(row_id.shape[0] > 0, column(f0), 1.0))
    w1 = jnp.where(row_id < modes, column(f1)[:ep], 1.0)
    w2 = jnp.where(lane < modes, f2, 1.0)
    occ = jnp.where(row_id < modes, column(d1)[:ep], 0.0) + jnp.where(lane < modes, d2, 0.0)
    inverse = 1.0 / (w1 * w2)

    for r in range(cl):
        got(0, 1, r)
    accumulate([(force_ref, 0), (blocks.at[0, 1], 1)], True)
    got(1, 0, 1)
    send(unit(1, 0, 1), unit(1, 1, 1), 1, 1, 1, sib)
    got(2, 0, 0)
    send(unit(2, 0, 0), unit(2, 1, 0), 2, 1, 0, sib)
    for k in (1, 2):
        for r in range(cl):
            got(k, 1, r)
    accumulate([(blocks.at[k, m], m) for k in (1, 2) for m in (0, 1)], False)
    got(3, 0, 0)
    send(unit(3, 0, 0), unit(3, 1, 0), 3, 1, 0, sib)
    got(3, 0, 1)
    send(unit(3, 0, 1), unit(3, 1, 1), 3, 1, 1, sib)
    got(3, 1, 0)
    got(3, 1, 1)
    accumulate([(blocks.at[3, 0], 0), (blocks.at[3, 1], 1)], False)

    for b in range(modes):
        part = zbuf[:, b * modes : (b + 1) * modes].astype(bf16)
        out = jnp.dot(part[:rp], e2a, preferred_element_type=f32) + jnp.dot(
            part[rp:], e2b, preferred_element_type=f32
        )
        tre[b * rp : (b + 1) * rp, :] = out[:, :LANES]
        tim[b * rp : (b + 1) * rp, :] = out[:, LANES:]
    tre[modes * rp :, :] = jnp.zeros(((ep - modes) * rp, LANES), f32)
    tim[modes * rp :, :] = jnp.zeros(((ep - modes) * rp, LANES), f32)

    scaled = 0.5 / (smearing * smearing)
    ratebuf[...] = jnp.zeros_like(ratebuf)
    coupbuf[...] = jnp.zeros_like(coupbuf)

    def modes_step(p, carry):
        def rows(ref):
            return jnp.concatenate(
                [ref[pl.ds(2 * p + i, ep, stride=rp), :] for i in range(2)], axis=1
            ).astype(bf16)

        amp = jnp.dot(left_a, rows(tre), preferred_element_type=f32) + jnp.dot(
            left_b, rows(tim), preferred_element_type=f32
        )
        square = amp * amp
        square = square[:ep] + square[ep:]
        for i in range(2):
            w0 = w0buf[pl.ds(2 * p + i, 1), :]
            decays = w0 - w1 - w2
            merges = w0 + w1 - w2
            gauss = jnp.exp(-scaled * decays * decays) + jnp.exp(-scaled * merges * merges)
            value = square[:, i * LANES : (i + 1) * LANES] * gauss * inverse
            ratebuf[pl.ds(2 * p + i, 1), :] = jnp.sum(value, axis=0, keepdims=True)
            coupbuf[pl.ds(2 * p + i, 1), :] = jnp.sum(value * occ, axis=0, keepdims=True)
        return carry

    lax.fori_loop(0, rp // 2, modes_step, 0)

    factor = mult_ref[me_c].astype(f32)
    w0_row = pick(me_m, [f0[:, m * half : (m + 1) * half] for m in range(n_mode)])
    rate = jnp.sum(jnp.transpose(ratebuf[...]), axis=0, keepdims=True)[:, :half] / w0_row * factor
    coup = jnp.sum(jnp.transpose(coupbuf[...]), axis=0, keepdims=True)[:, :half] / w0_row * factor
    msg[...] = jnp.zeros_like(msg)
    msg[0:1, 0:half] = rate
    msg[1:2, 0:half] = coup
    msg[2:3, :] = jnp.full((1, LANES), irr_ref[me_c].astype(f32))

    copies = []
    for index, (dt, dc) in enumerate(peers):
        copy = pltpu.make_async_remote_copy(
            src_ref=msg,
            dst_ref=inbox.at[index],
            send_sem=m_send.at[index],
            recv_sem=m_recv.at[index],
            device_id=peer_id(dt, dc),
            device_id_type=MESH,
        )
        copy.start()
        copies.append(copy)
    for copy in started:
        copy.wait_send()
    for copy in copies:
        copy.wait()

    nq = gamma_ref.shape[0]
    for q in range(nq):
        name = (me_t * nq + q).astype(f32)

        def kept(tile):
            return jnp.where(tile[2:3, :half] == name, tile[0:2, :half], 0.0)

        total = kept(msg[...])
        if len(peers) <= 16:
            for index in range(len(peers)):
                total = total + kept(inbox[index])
        else:
            total = lax.fori_loop(0, len(peers), lambda i, acc: acc + kept(inbox[i]), total)
        gamma = total[0:1] + bound_ref[q : q + 1, :]
        gamma_ref[q : q + 1, :] = gamma
        dev_ref[q : q + 1, :] = (drive_ref[q : q + 1, :] + total[1:2]) / gamma


def body(
    force_third,
    phase_angle,
    eigenvectors,
    frequencies,
    deviation,
    send_rows,
    trip_table,
    irreducible,
    multiplicity,
    drive_term,
    boundary,
):
    n_clus, n_trip, n_mode = (lax.axis_size(name) for name in ("clus", "trip", "mode"))
    cl, half, flat = force_third.shape
    points, modes, _ = eigenvectors.shape
    slot = send_rows.shape[1] // n_trip
    chunk = 512
    rp = up(half + 2, 16)
    ep = up(modes + 1, 16)
    npad = up(flat, chunk)
    angles = phase_angle.astype(f32)
    trig = jnp.stack([jnp.cos(angles), jnp.sin(angles)], axis=1).astype(bf16)
    tail = jnp.pad(trig, ((0, 0), (0, rp - half - 2), (0, npad - trig.shape[2])))
    force = jnp.concatenate(
        [jnp.pad(force_third, ((0, 0), (0, 0), (0, npad - flat))), tail], axis=1
    ).reshape(cl * rp, npad)
    first = lax.axis_index("mode") == 0
    part = jnp.where(first, eigenvectors[..., :modes], eigenvectors[..., modes:])
    extra = jnp.where(first, frequencies, deviation)[:, None]
    eig = jnp.pad(
        jnp.concatenate([part, extra], axis=1),
        ((0, 0), (0, ep - modes - 1), (0, LANES - modes)),
    )
    n_peers = n_clus * n_trip - 1
    vmem = pl.BlockSpec(memory_space=pltpu.VMEM)
    smem = pl.BlockSpec(memory_space=pltpu.SMEM)
    out = jax.ShapeDtypeStruct(boundary.shape, f32)
    dma = pltpu.SemaphoreType.DMA
    return tuple(
        pl.pallas_call(
            functools.partial(
                kernel, (n_clus, n_trip, n_mode, modes, half, rp, cl, slot, chunk)
            ),
            out_shape=(out, out),
            in_specs=[vmem, vmem, smem, smem, smem, smem, vmem, vmem],
            out_specs=(vmem, vmem),
            scratch_shapes=[
                pltpu.VMEM((n_clus, n_mode, cl * rp, npad), bf16),
                pltpu.VMEM((n_trip, slot, ep, LANES), bf16),
                pltpu.VMEM((n_trip, slot, ep, LANES), bf16),
                pltpu.VMEM((3, ep, LANES), bf16),
                pltpu.VMEM((3, ep, LANES), bf16),
                pltpu.VMEM((2 * rp, npad), f32),
                pltpu.VMEM((ep * rp, LANES), f32),
                pltpu.VMEM((ep * rp, LANES), f32),
                pltpu.VMEM((rp, LANES), f32),
                pltpu.VMEM((LANES, LANES), f32),
                pltpu.VMEM((LANES, LANES), f32),
                pltpu.VMEM((8, LANES), f32),
                pltpu.VMEM((n_peers, 8, LANES), f32),
                dma((n_clus, n_mode, cl)),
                dma((n_clus, n_mode, cl)),
                dma((n_trip,)),
                dma((n_trip,)),
                dma,
                dma,
                dma((n_peers,)),
                dma((n_peers,)),
            ],
            compiler_params=pltpu.CompilerParams(
                collective_id=0, has_side_effects=True, vmem_limit_bytes=48 * 1024 * 1024
            ),
        )(force, eig, send_rows, trip_table, irreducible, multiplicity, drive_term, boundary)
    )


def solution(mesh):
    return jax.shard_map(
        body,
        mesh=mesh,
        in_specs=(
            P("clus", "mode", None),
            P("clus", "trip"),
            P("trip", None, None),
            P("trip", None),
            P("trip", None),
            P("trip", None),
            P("trip", None),
            P("trip"),
            P("trip"),
            P("trip", "mode"),
            P("trip", "mode"),
        ),
        out_specs=(P("trip", "mode"), P("trip", "mode")),
        check_vma=False,
    )
```

```python
import functools

import jax
import jax.numpy as jnp
from jax import lax
from jax.experimental import pallas as pl
from jax.experimental.pallas import tpu as pltpu
from jax.sharding import PartitionSpec as P

smearing = 0.3
MESH = pl.DeviceIdType.MESH
LANES = 128
f32 = jnp.float32
bf16 = jnp.bfloat16


def up(value, step):
    return -(-value // step) * step


def pick(index, options):
    chosen = options[0]
    for position in range(1, len(options)):
        chosen = jnp.where(index == position, options[position], chosen)
    return chosen


def kernel(
    dims,
    force_ref,
    tail_ref,
    eig_ref,
    send_rows_ref,
    table_ref,
    irr_ref,
    mult_ref,
    drive_ref,
    bound_ref,
    gamma_ref,
    dev_ref,
    blocks,
    tails,
    wbuf,
    left,
    asked,
    wanted,
    outgoing,
    arrived,
    mine,
    other,
    zbuf,
    tre,
    tim,
    w0buf,
    ratebuf,
    coupbuf,
    msg,
    inbox,
    f_send,
    f_recv,
    t_send,
    t_recv,
    c_send,
    c_recv,
    e_send,
    e_recv,
    p_send,
    p_recv,
    m_send,
    m_recv,
):
    n_clus, n_trip, n_mode, modes, half, rp, cl, slot, wide = dims
    ep = eig_ref.shape[1]
    flat = force_ref.shape[2]
    unit_rows = cl * rp
    chunks = zbuf.shape[1] // wide
    me_c = lax.axis_index("clus")
    me_t = lax.axis_index("trip")
    me_m = lax.axis_index("mode")
    sib = (me_c, me_t, 1 - me_m)
    odd = lax.rem(me_t, 2)
    low, high = lax.rem(me_c, 2), me_c // 2
    near = (me_c + (1 - odd) * (1 - 2 * low) + odd * (2 - 4 * high), me_t, me_m)
    far = (me_c + odd * (1 - 2 * low) + (1 - odd) * (2 - 4 * high), me_t, me_m)
    plane = (me_c, me_t + 1 - 2 * odd, me_m)

    peers = []
    for dt in range(n_trip):
        for dc in range(n_clus):
            if dt or dc:
                peers.append((dt, dc))

    def peer_id(dt, dc):
        return (lax.rem(me_c + dc, n_clus), lax.rem(me_t + dt, n_trip), me_m)

    barrier = pltpu.get_barrier_semaphore()
    for dt, dc in peers:
        pl.semaphore_signal(barrier, inc=1, device_id=peer_id(dt, dc), device_id_type=MESH)
    pl.semaphore_signal(barrier, inc=1, device_id=sib, device_id_type=MESH)

    asked[...] = jnp.zeros_like(asked)
    for j in range(3):
        asked[j : j + 1, :] = jnp.full((1, LANES), table_ref[me_c, j].astype(f32))

    whole = half // 16 * 16
    for n in range(chunks):
        lo = n * wide
        hi = min(lo + wide, flat)
        for r in range(cl):
            at = r * rp
            if hi < lo + wide:
                edge = hi // LANES * LANES
                blocks[at : at + rp, edge : lo + wide] = jnp.zeros((rp, lo + wide - edge), bf16)
            blocks[at : at + whole, lo:hi] = force_ref[r, :whole, lo:hi]
            rest = force_ref[r, whole:, lo:hi].astype(f32)
            under = jnp.zeros((rp - half, hi - lo), f32)
            blocks[at + whole : at + rp, lo:hi] = jnp.concatenate([rest, under], axis=0).astype(bf16)

    pl.semaphore_wait(barrier, len(peers) + 1)

    def unit(k, m, n):
        return blocks.at[pl.ds((k * 2 + m) * unit_rows, unit_rows), pl.ds(n * wide, wide)]

    started = []

    def copy_of(src, k, m, n, device):
        return pltpu.make_async_remote_copy(
            src_ref=src,
            dst_ref=unit(k, m, n),
            send_sem=f_send.at[k, m, n],
            recv_sem=f_recv.at[k, m, n],
            device_id=device,
            device_id_type=MESH,
        )

    def send(src, k, m, n, device):
        copy = copy_of(src, k, m, n, device)
        copy.start()
        started.append(copy)

    def got(k, m, n):
        copy_of(unit(k, m, n), k, m, n, sib).wait_recv()

    asks = []
    for dt in range(1, n_trip):
        copy = pltpu.make_async_remote_copy(
            src_ref=asked,
            dst_ref=wanted.at[dt],
            send_sem=t_send.at[dt],
            recv_sem=t_recv.at[dt],
            device_id=(me_c, lax.rem(me_t + dt, n_trip), me_m),
            device_id_type=MESH,
        )
        copy.start()
        asks.append(copy)
    phase_copies = []
    for k, device in ((1, near), (2, far), (3, (3 - me_c, me_t, me_m))):
        copy = pltpu.make_async_remote_copy(
            src_ref=tail_ref,
            dst_ref=tails.at[k],
            send_sem=c_send.at[k],
            recv_sem=c_recv.at[k],
            device_id=device,
            device_id_type=MESH,
        )
        copy.start()
        phase_copies.append(copy)
    for n in range(chunks):
        send(unit(0, 0, n), 1, 0, n, near)
    for n in range(chunks):
        send(unit(0, 0, n), 0, 1, n, sib)

    def answer(dt, wishes):
        target = lax.rem(me_t - dt + n_trip, n_trip)
        for j in range(3):
            wish = wishes[j : j + 1, :]
            block = jnp.zeros((ep, LANES), f32)
            for k in range(slot):
                row = send_rows_ref[0, target * slot + k]
                name = (me_t * slot + k).astype(f32)
                block = jnp.where(wish == name, eig_ref[row].astype(f32), block)
            outgoing[dt, j] = block.astype(bf16)

    answer(0, asked[...])
    eig_copies = []
    for dt in range(1, n_trip):
        asks[dt - 1].wait()
        answer(dt, wanted[dt])
    for dt in range(1, n_trip):
        copy = pltpu.make_async_remote_copy(
            src_ref=outgoing.at[dt],
            dst_ref=arrived.at[dt],
            send_sem=e_send.at[dt],
            recv_sem=e_recv.at[dt],
            device_id=(me_c, lax.rem(me_t - dt + n_trip, n_trip), me_m),
            device_id_type=MESH,
        )
        copy.start()
        eig_copies.append(copy)
    arrived[0] = outgoing[0]

    def direct(n):
        got(1, 0, n)
        send(unit(1, 0, n), 2, 0, n, plane)
        send(unit(1, 0, n), 3, 0, n, far)
        send(unit(1, 0, n), 1, 1, n, sib)

    def second(n):
        got(2, 0, n)
        send(unit(2, 0, n), 2, 1, n, sib)
        got(3, 0, n)
        send(unit(3, 0, n), 3, 1, n, sib)

    direct(0)
    for copy in eig_copies:
        copy.wait()
    for j in range(3):
        source = table_ref[me_c, j] // slot
        mine[j] = arrived[lax.rem(source - me_t + n_trip, n_trip), j]
    pair = pltpu.make_async_remote_copy(
        src_ref=mine,
        dst_ref=other,
        send_sem=p_send,
        recv_sem=p_recv,
        device_id=sib,
        device_id_type=MESH,
    )
    pair.start()
    direct(1)
    pair.wait()

    first = me_m == 0

    def complex_of(j):
        a = mine[j].astype(f32)
        b = other[j].astype(f32)
        return jnp.where(first, a, b), jnp.where(first, b, a)

    re0, im0 = complex_of(0)
    re1, im1 = complex_of(1)
    re2, im2 = complex_of(2)
    f0 = re0[modes : modes + 1]
    f1, d1 = re1[modes : modes + 1], im1[modes : modes + 1]
    f2, d2 = re2[modes : modes + 1], im2[modes : modes + 1]

    def half_rows(mat):
        return pick(me_m, [mat[m * half : m * half + rp] for m in range(n_mode)])

    fill = jnp.zeros((rp - half, LANES), f32)

    def lead(mat, m):
        part = mat[m * half : (m + 1) * half]
        stacked = jnp.concatenate([part, fill] * cl, axis=0)
        return half_rows(jnp.transpose(stacked))

    lead_re = [lead(re0, m) for m in range(n_mode)]
    lead_im = [lead(im0, m) for m in range(n_mode)]
    lane_k = lax.broadcasted_iota(jnp.int32, (rp, cl * rp), 1)
    lane = lax.broadcasted_iota(jnp.int32, (1, LANES), 1)

    def weights(k):
        cosines, sines = [], []
        for r in range(cl):
            tail = tail_ref[r] if k == 0 else tails[k, r]
            cosines.append(jnp.sum(jnp.where(lane == me_c, tail[0:1], 0.0), axis=1, keepdims=True))
            sines.append(jnp.sum(jnp.where(lane == me_c, tail[1:2], 0.0), axis=1, keepdims=True))
        cosv, sinv = cosines[0], sines[0]
        for r in range(1, cl):
            cosv = jnp.where(lane_k >= r * rp, cosines[r], cosv)
            sinv = jnp.where(lane_k >= r * rp, sines[r], sinv)
        for m in range(2):
            wre = jnp.where(first, lead_re[m], lead_re[1 - m])
            wim = jnp.where(first, lead_im[m], lead_im[1 - m])
            at = (k * 2 + m) * unit_rows
            wbuf[:, at : at + unit_rows] = jnp.concatenate(
                [cosv * wre - sinv * wim, cosv * wim + sinv * wre], axis=0
            ).astype(bf16)

    e2a = jnp.concatenate([re2, im2], axis=1)[:modes].astype(bf16)
    e2b = jnp.concatenate([-im2, re2], axis=1)[:modes].astype(bf16)
    row_id = lax.broadcasted_iota(jnp.int32, (ep, LANES), 0)
    e1re_t = jnp.transpose(jnp.where(row_id < modes, re1, 0.0))[:ep]
    e1im_t = jnp.transpose(jnp.where(row_id < modes, im1, 0.0))[:ep]
    left[:, :ep] = jnp.concatenate([e1re_t, e1im_t], axis=0).astype(bf16)
    left[:, ep:] = jnp.concatenate([-e1im_t, e1re_t], axis=0).astype(bf16)

    def column(row):
        return jnp.transpose(jnp.broadcast_to(row, (LANES, LANES)))

    w0buf[...] = half_rows(column(f0))
    w1 = jnp.where(row_id < modes, column(f1)[:ep], 1.0)
    w2 = jnp.where(lane < modes, f2, 1.0)
    occ = jnp.where(row_id < modes, column(d1)[:ep], 0.0) + jnp.where(lane < modes, d2, 0.0)
    inverse = 1.0 / (w1 * w2)
    tre[modes * rp :, :] = jnp.zeros(((ep - modes) * rp, LANES), f32)
    tim[modes * rp :, :] = jnp.zeros(((ep - modes) * rp, LANES), f32)

    def contract(n):
        for k in range(4):
            got(k, 1, n)
        step = wide // 2
        for i in range(2):
            cols = slice(n * wide + i * step, n * wide + (i + 1) * step)
            zbuf[:, cols] = jnp.dot(wbuf[...], blocks[:, cols], preferred_element_type=f32)
        for b in range(modes):
            if not n * wide < (b + 1) * modes <= (n + 1) * wide:
                continue
            part = zbuf[:, b * modes : (b + 1) * modes].astype(bf16)
            out = jnp.dot(part[:rp], e2a, preferred_element_type=f32) + jnp.dot(
                part[rp:], e2b, preferred_element_type=f32
            )
            tre[b * rp : (b + 1) * rp, :] = out[:, :LANES]
            tim[b * rp : (b + 1) * rp, :] = out[:, LANES:]

    for copy in phase_copies:
        copy.wait()
    for k in range(4):
        weights(k)

    for n in range(2, chunks + 3):
        if n < chunks:
            direct(n)
        if 0 <= n - 2 < chunks:
            second(n - 2)
        if 0 <= n - 3 < chunks:
            contract(n - 3)

    scaled = 0.5 / (smearing * smearing)
    ratebuf[...] = jnp.zeros_like(ratebuf)
    coupbuf[...] = jnp.zeros_like(coupbuf)

    def modes_step(p, carry):
        def rows(ref):
            return jnp.concatenate(
                [ref[pl.ds(2 * p + i, ep, stride=rp), :] for i in range(2)], axis=1
            ).astype(bf16)

        both = jnp.concatenate([rows(tre), rows(tim)], axis=0)
        amp = jnp.dot(left[...], both, preferred_element_type=f32)
        square = amp * amp
        square = square[:ep] + square[ep:]
        for i in range(2):
            w0 = w0buf[pl.ds(2 * p + i, 1), :]
            decays = w0 - w1 - w2
            merges = w0 + w1 - w2
            gauss = jnp.exp(-scaled * decays * decays) + jnp.exp(-scaled * merges * merges)
            value = square[:, i * LANES : (i + 1) * LANES] * gauss * inverse
            ratebuf[pl.ds(2 * p + i, 1), :] = jnp.sum(value, axis=0, keepdims=True)
            coupbuf[pl.ds(2 * p + i, 1), :] = jnp.sum(value * occ, axis=0, keepdims=True)
        return carry

    lax.fori_loop(0, up(half, 2) // 2, modes_step, 0)

    factor = mult_ref[me_c].astype(f32)
    w0_row = pick(me_m, [f0[:, m * half : (m + 1) * half] for m in range(n_mode)])
    rate = jnp.sum(jnp.transpose(ratebuf[...]), axis=0, keepdims=True)[:, :half] / w0_row * factor
    coup = jnp.sum(jnp.transpose(coupbuf[...]), axis=0, keepdims=True)[:, :half] / w0_row * factor
    msg[...] = jnp.zeros_like(msg)
    msg[0:1, 0:half] = rate
    msg[1:2, 0:half] = coup
    msg[2:3, :] = jnp.full((1, LANES), irr_ref[me_c].astype(f32))

    copies = []
    for index, (dt, dc) in enumerate(peers):
        copy = pltpu.make_async_remote_copy(
            src_ref=msg,
            dst_ref=inbox.at[index],
            send_sem=m_send.at[index],
            recv_sem=m_recv.at[index],
            device_id=peer_id(dt, dc),
            device_id_type=MESH,
        )
        copy.start()
        copies.append(copy)
    for copy in started:
        copy.wait_send()
    for copy in copies:
        copy.wait()

    nq = gamma_ref.shape[0]
    for q in range(nq):
        name = (me_t * nq + q).astype(f32)

        def kept(tile):
            return jnp.where(tile[2:3, :half] == name, tile[0:2, :half], 0.0)

        total = kept(msg[...])
        if len(peers) <= 16:
            for index in range(len(peers)):
                total = total + kept(inbox[index])
        else:
            total = lax.fori_loop(0, len(peers), lambda i, acc: acc + kept(inbox[i]), total)
        gamma = total[0:1] + bound_ref[q : q + 1, :]
        gamma_ref[q : q + 1, :] = gamma
        dev_ref[q : q + 1, :] = (drive_ref[q : q + 1, :] + total[1:2]) / gamma


def body(
    force_third,
    phase_angle,
    eigenvectors,
    frequencies,
    deviation,
    send_rows,
    trip_table,
    irreducible,
    multiplicity,
    drive_term,
    boundary,
):
    n_clus, n_trip, n_mode = (lax.axis_size(name) for name in ("clus", "trip", "mode"))
    cl, half, flat = force_third.shape
    points, modes, _ = eigenvectors.shape
    slot = send_rows.shape[1] // n_trip
    wide = 1024
    rp = up(half, 16)
    ep = up(modes + 1, 16)
    npad = up(flat, wide)
    chunks = npad // wide
    angles = phase_angle.astype(f32)
    trig = jnp.stack([jnp.cos(angles), jnp.sin(angles)], axis=1).astype(bf16).astype(f32)
    tail = jnp.pad(trig, ((0, 0), (0, 6), (0, LANES - trig.shape[2])))
    first = lax.axis_index("mode") == 0
    part = jnp.where(first, eigenvectors[..., :modes], eigenvectors[..., modes:])
    extra = jnp.where(first, frequencies, deviation)[:, None]
    eig = jnp.pad(
        jnp.concatenate([part, extra], axis=1),
        ((0, 0), (0, ep - modes - 1), (0, LANES - modes)),
    )
    n_peers = n_clus * n_trip - 1
    vmem = pl.BlockSpec(memory_space=pltpu.VMEM)
    smem = pl.BlockSpec(memory_space=pltpu.SMEM)
    out = jax.ShapeDtypeStruct(boundary.shape, f32)
    dma = pltpu.SemaphoreType.DMA
    return tuple(
        pl.pallas_call(
            functools.partial(
                kernel, (n_clus, n_trip, n_mode, modes, half, rp, cl, slot, wide)
            ),
            out_shape=(out, out),
            in_specs=[vmem, vmem, vmem, smem, smem, smem, smem, vmem, vmem],
            out_specs=(vmem, vmem),
            scratch_shapes=[
                pltpu.VMEM((n_clus * n_mode * cl * rp, npad), bf16),
                pltpu.VMEM((n_clus, cl, 8, LANES), f32),
                pltpu.VMEM((2 * rp, n_clus * n_mode * cl * rp), bf16),
                pltpu.VMEM((2 * ep, 2 * ep), bf16),
                pltpu.VMEM((8, LANES), f32),
                pltpu.VMEM((n_trip, 8, LANES), f32),
                pltpu.VMEM((n_trip, 3, ep, LANES), bf16),
                pltpu.VMEM((n_trip, 3, ep, LANES), bf16),
                pltpu.VMEM((3, ep, LANES), bf16),
                pltpu.VMEM((3, ep, LANES), bf16),
                pltpu.VMEM((2 * rp, npad), f32),
                pltpu.VMEM((ep * rp, LANES), f32),
                pltpu.VMEM((ep * rp, LANES), f32),
                pltpu.VMEM((rp, LANES), f32),
                pltpu.VMEM((LANES, LANES), f32),
                pltpu.VMEM((LANES, LANES), f32),
                pltpu.VMEM((8, LANES), f32),
                pltpu.VMEM((n_peers, 8, LANES), f32),
                dma((n_clus, n_mode, chunks)),
                dma((n_clus, n_mode, chunks)),
                dma((n_trip,)),
                dma((n_trip,)),
                dma((n_clus,)),
                dma((n_clus,)),
                dma((n_trip,)),
                dma((n_trip,)),
                dma,
                dma,
                dma((n_peers,)),
                dma((n_peers,)),
            ],
            compiler_params=pltpu.CompilerParams(
                collective_id=0, has_side_effects=True, vmem_limit_bytes=48 * 1024 * 1024
            ),
        )(force_third, tail, eig, send_rows, trip_table, irreducible, multiplicity, drive_term, boundary)
    )


def solution(mesh):
    return jax.shard_map(
        body,
        mesh=mesh,
        in_specs=(
            P("clus", "mode", None),
            P("clus", "trip"),
            P("trip", None, None),
            P("trip", None),
            P("trip", None),
            P("trip", None),
            P("trip", None),
            P("trip"),
            P("trip"),
            P("trip", "mode"),
            P("trip", "mode"),
        ),
        out_specs=(P("trip", "mode"), P("trip", "mode")),
        check_vma=False,
    )
```

```python
import functools

import jax
import jax.numpy as jnp
from jax import lax
from jax.experimental import pallas as pl
from jax.experimental.pallas import tpu as pltpu
from jax.sharding import PartitionSpec as P

smearing = 0.3
MESH = pl.DeviceIdType.MESH
LANES = 128
f32 = jnp.float32
bf16 = jnp.bfloat16


def up(value, step):
    return -(-value // step) * step


def pick(index, options):
    chosen = options[0]
    for position in range(1, len(options)):
        chosen = jnp.where(index == position, options[position], chosen)
    return chosen


def kernel(
    dims,
    force_ref,
    tail_ref,
    eig_ref,
    send_rows_ref,
    table_ref,
    irr_ref,
    mult_ref,
    drive_ref,
    bound_ref,
    gamma_ref,
    dev_ref,
    blocks,
    tails,
    wbuf,
    left,
    asked,
    wanted,
    outgoing,
    arrived,
    mine,
    other,
    zbuf,
    tre,
    tim,
    w0buf,
    ratebuf,
    coupbuf,
    msg,
    inbox,
    f_send,
    f_recv,
    t_send,
    t_recv,
    c_send,
    c_recv,
    e_send,
    e_recv,
    p_send,
    p_recv,
    m_send,
    m_recv,
):
    n_clus, n_trip, n_mode, modes, half, rp, cl, slot, wide = dims
    ep = eig_ref.shape[1]
    flat = force_ref.shape[2]
    unit_rows = cl * rp
    chunks = zbuf.shape[1] // wide
    me_c = lax.axis_index("clus")
    me_t = lax.axis_index("trip")
    me_m = lax.axis_index("mode")
    sib = (me_c, me_t, 1 - me_m)
    odd = lax.rem(me_t, 2)
    low, high = lax.rem(me_c, 2), me_c // 2
    near = (me_c + (1 - odd) * (1 - 2 * low) + odd * (2 - 4 * high), me_t, me_m)
    far = (me_c + odd * (1 - 2 * low) + (1 - odd) * (2 - 4 * high), me_t, me_m)
    plane = (me_c, me_t + 1 - 2 * odd, me_m)

    peers = []
    for dt in range(n_trip):
        for dc in range(n_clus):
            if dt or dc:
                peers.append((dt, dc))

    def peer_id(dt, dc):
        return (lax.rem(me_c + dc, n_clus), lax.rem(me_t + dt, n_trip), me_m)

    barrier = pltpu.get_barrier_semaphore()
    for dt, dc in peers:
        pl.semaphore_signal(barrier, inc=1, device_id=peer_id(dt, dc), device_id_type=MESH)
    pl.semaphore_signal(barrier, inc=1, device_id=sib, device_id_type=MESH)

    asked[...] = jnp.zeros_like(asked)
    for j in range(3):
        asked[j : j + 1, :] = jnp.full((1, LANES), table_ref[me_c, j].astype(f32))

    whole = half // 16 * 16
    for n in range(chunks):
        lo = n * wide
        hi = min(lo + wide, flat)
        for r in range(cl):
            at = r * rp
            if hi < lo + wide:
                edge = hi // LANES * LANES
                blocks[at : at + rp, edge : lo + wide] = jnp.zeros((rp, lo + wide - edge), bf16)
            blocks[at : at + whole, lo:hi] = force_ref[r, :whole, lo:hi]
            rest = force_ref[r, whole:, lo:hi].astype(f32)
            under = jnp.zeros((rp - half, hi - lo), f32)
            blocks[at + whole : at + rp, lo:hi] = jnp.concatenate([rest, under], axis=0).astype(bf16)

    pl.semaphore_wait(barrier, len(peers) + 1)

    def unit(k, m, n):
        return blocks.at[pl.ds((k * 2 + m) * unit_rows, unit_rows), pl.ds(n * wide, wide)]

    started = []

    def copy_of(src, k, m, n, device):
        return pltpu.make_async_remote_copy(
            src_ref=src,
            dst_ref=unit(k, m, n),
            send_sem=f_send.at[k, m, n],
            recv_sem=f_recv.at[k, m, n],
            device_id=device,
            device_id_type=MESH,
        )

    def send(src, k, m, n, device):
        copy = copy_of(src, k, m, n, device)
        copy.start()
        started.append(copy)

    def got(k, m, n):
        copy_of(unit(k, m, n), k, m, n, sib).wait_recv()

    asks = []
    for dt in range(1, n_trip):
        copy = pltpu.make_async_remote_copy(
            src_ref=asked,
            dst_ref=wanted.at[dt],
            send_sem=t_send.at[dt],
            recv_sem=t_recv.at[dt],
            device_id=(me_c, lax.rem(me_t + dt, n_trip), me_m),
            device_id_type=MESH,
        )
        copy.start()
        asks.append(copy)
    phase_copies = []
    for k, device in ((1, near), (2, far), (3, (3 - me_c, me_t, me_m))):
        copy = pltpu.make_async_remote_copy(
            src_ref=tail_ref,
            dst_ref=tails.at[k],
            send_sem=c_send.at[k],
            recv_sem=c_recv.at[k],
            device_id=device,
            device_id_type=MESH,
        )
        copy.start()
        phase_copies.append(copy)
    for n in range(chunks):
        send(unit(0, 0, n), 1, 0, n, near)
    for n in range(chunks):
        send(unit(0, 0, n), 0, 1, n, sib)

    def answer(dt, wishes):
        target = lax.rem(me_t - dt + n_trip, n_trip)
        for j in range(3):
            wish = wishes[j : j + 1, :]
            block = jnp.zeros((ep, LANES), f32)
            for k in range(slot):
                row = send_rows_ref[0, target * slot + k]
                name = (me_t * slot + k).astype(f32)
                block = jnp.where(wish == name, eig_ref[row].astype(f32), block)
            outgoing[dt, j] = block.astype(bf16)

    answer(0, asked[...])
    eig_copies = []
    for dt in range(1, n_trip):
        asks[dt - 1].wait()
        answer(dt, wanted[dt])
    for dt in range(1, n_trip):
        copy = pltpu.make_async_remote_copy(
            src_ref=outgoing.at[dt],
            dst_ref=arrived.at[dt],
            send_sem=e_send.at[dt],
            recv_sem=e_recv.at[dt],
            device_id=(me_c, lax.rem(me_t - dt + n_trip, n_trip), me_m),
            device_id_type=MESH,
        )
        copy.start()
        eig_copies.append(copy)
    arrived[0] = outgoing[0]

    def direct(n):
        got(1, 0, n)
        send(unit(1, 0, n), 2, 0, n, plane)
        send(unit(1, 0, n), 3, 0, n, far)
        send(unit(1, 0, n), 1, 1, n, sib)

    def second(n):
        got(2, 0, n)
        send(unit(2, 0, n), 2, 1, n, sib)
        got(3, 0, n)
        send(unit(3, 0, n), 3, 1, n, sib)

    direct(0)
    for copy in eig_copies:
        copy.wait()
    for j in range(3):
        source = table_ref[me_c, j] // slot
        mine[j] = arrived[lax.rem(source - me_t + n_trip, n_trip), j]
    pair = pltpu.make_async_remote_copy(
        src_ref=mine,
        dst_ref=other,
        send_sem=p_send,
        recv_sem=p_recv,
        device_id=sib,
        device_id_type=MESH,
    )
    pair.start()
    direct(1)
    pair.wait()

    first = me_m == 0

    def complex_of(j):
        a = mine[j].astype(f32)
        b = other[j].astype(f32)
        return jnp.where(first, a, b), jnp.where(first, b, a)

    re0, im0 = complex_of(0)
    re1, im1 = complex_of(1)
    re2, im2 = complex_of(2)
    f0 = re0[modes : modes + 1]
    f1, d1 = re1[modes : modes + 1], im1[modes : modes + 1]
    f2, d2 = re2[modes : modes + 1], im2[modes : modes + 1]

    def half_rows(mat):
        return pick(me_m, [mat[m * half : m * half + rp] for m in range(n_mode)])

    fill = jnp.zeros((rp - half, LANES), f32)

    def lead(mat, m):
        part = mat[m * half : (m + 1) * half]
        stacked = jnp.concatenate([part, fill] * cl, axis=0)
        return half_rows(jnp.transpose(stacked))

    lead_re = [lead(re0, m) for m in range(n_mode)]
    lead_im = [lead(im0, m) for m in range(n_mode)]
    lane_k = lax.broadcasted_iota(jnp.int32, (rp, cl * rp), 1)
    lane = lax.broadcasted_iota(jnp.int32, (1, LANES), 1)

    def weights(k):
        cosines, sines = [], []
        for r in range(cl):
            tail = tail_ref[r] if k == 0 else tails[k, r]
            cosines.append(jnp.sum(jnp.where(lane == me_c, tail[0:1], 0.0), axis=1, keepdims=True))
            sines.append(jnp.sum(jnp.where(lane == me_c, tail[1:2], 0.0), axis=1, keepdims=True))
        cosv, sinv = cosines[0], sines[0]
        for r in range(1, cl):
            cosv = jnp.where(lane_k >= r * rp, cosines[r], cosv)
            sinv = jnp.where(lane_k >= r * rp, sines[r], sinv)
        for m in range(2):
            wre = jnp.where(first, lead_re[m], lead_re[1 - m])
            wim = jnp.where(first, lead_im[m], lead_im[1 - m])
            at = (k * 2 + m) * unit_rows
            wbuf[:, at : at + unit_rows] = jnp.concatenate(
                [cosv * wre - sinv * wim, cosv * wim + sinv * wre], axis=0
            ).astype(bf16)

    e2a = jnp.concatenate([re2, im2], axis=1)[:modes].astype(bf16)
    e2b = jnp.concatenate([-im2, re2], axis=1)[:modes].astype(bf16)
    row_id = lax.broadcasted_iota(jnp.int32, (ep, LANES), 0)
    e1re_t = jnp.transpose(jnp.where(row_id < modes, re1, 0.0))[:ep]
    e1im_t = jnp.transpose(jnp.where(row_id < modes, im1, 0.0))[:ep]
    left[:, :ep] = jnp.concatenate([e1re_t, e1im_t], axis=0).astype(bf16)
    left[:, ep:] = jnp.concatenate([-e1im_t, e1re_t], axis=0).astype(bf16)

    def column(row):
        return jnp.transpose(jnp.broadcast_to(row, (LANES, LANES)))

    w0buf[...] = half_rows(column(f0))
    w1 = jnp.where(row_id < modes, column(f1)[:ep], 1.0)
    w2 = jnp.where(lane < modes, f2, 1.0)
    occ = jnp.where(row_id < modes, column(d1)[:ep], 0.0) + jnp.where(lane < modes, d2, 0.0)
    inverse = 1.0 / (w1 * w2)
    tre[modes * rp :, :] = jnp.zeros(((ep - modes) * rp, LANES), f32)
    tim[modes * rp :, :] = jnp.zeros(((ep - modes) * rp, LANES), f32)

    def contract(n):
        for k in range(4):
            got(k, 1, n)
        cols = slice(n * wide, (n + 1) * wide)
        zbuf[:, cols] = jnp.dot(wbuf[...], blocks[:, cols], preferred_element_type=f32)
        for b in range(modes):
            if not n * wide < (b + 1) * modes <= (n + 1) * wide:
                continue
            part = zbuf[:, b * modes : (b + 1) * modes].astype(bf16)
            out = jnp.dot(part[:rp], e2a, preferred_element_type=f32) + jnp.dot(
                part[rp:], e2b, preferred_element_type=f32
            )
            tre[b * rp : (b + 1) * rp, :] = out[:, :LANES]
            tim[b * rp : (b + 1) * rp, :] = out[:, LANES:]

    for copy in phase_copies:
        copy.wait()
    for k in range(4):
        weights(k)

    for n in range(2, chunks + 3):
        if n < chunks:
            direct(n)
        if 0 <= n - 2 < chunks:
            second(n - 2)
        if 0 <= n - 3 < chunks:
            contract(n - 3)

    scaled = 0.5 / (smearing * smearing)
    lower = w1 + w2
    upper = w1 - w2

    def one_pair(s0):
        def rows(ref):
            return jnp.concatenate(
                [ref[pl.ds(s0 + i, ep, stride=rp), :] for i in range(2)], axis=1
            ).astype(bf16)

        both = jnp.concatenate([rows(tre), rows(tim)], axis=0)
        amp = jnp.dot(left[...], both, preferred_element_type=f32)
        square = amp * amp
        square = square[:ep] + square[ep:]
        for i in range(2):
            w0 = w0buf[pl.ds(s0 + i, 1), :]
            decays = w0 - lower
            merges = w0 + upper
            gauss = jnp.exp(-scaled * (decays * decays)) + jnp.exp(-scaled * (merges * merges))
            value = square[:, i * LANES : (i + 1) * LANES] * gauss * inverse
            at = pl.ds(pl.multiple_of((s0 + i) * 8, 8), 8)
            ratebuf[at, :] = jnp.sum(value.reshape(ep // 8, 8, LANES), axis=0)
            coupbuf[at, :] = jnp.sum((value * occ).reshape(ep // 8, 8, LANES), axis=0)

    group = 4

    def modes_step(p, carry):
        for i in range(group):
            one_pair((p * group + i) * 2)
        return carry

    lax.fori_loop(0, rp // (2 * group), modes_step, 0)

    def folded(ref):
        total = ref[pl.ds(0, rp, stride=8), :]
        for i in range(1, 8):
            total = total + ref[pl.ds(i, rp, stride=8), :]
        return jnp.sum(jnp.transpose(total), axis=0, keepdims=True)[:, :half]

    factor = mult_ref[me_c].astype(f32)
    w0_row = pick(me_m, [f0[:, m * half : (m + 1) * half] for m in range(n_mode)])
    rate = folded(ratebuf) / w0_row * factor
    coup = folded(coupbuf) / w0_row * factor
    msg[...] = jnp.zeros_like(msg)
    msg[0:1, 0:half] = rate
    msg[1:2, 0:half] = coup
    msg[2:3, :] = jnp.full((1, LANES), irr_ref[me_c].astype(f32))

    copies = []
    for index, (dt, dc) in enumerate(peers):
        copy = pltpu.make_async_remote_copy(
            src_ref=msg,
            dst_ref=inbox.at[index],
            send_sem=m_send.at[index],
            recv_sem=m_recv.at[index],
            device_id=peer_id(dt, dc),
            device_id_type=MESH,
        )
        copy.start()
        copies.append(copy)
    for copy in started:
        copy.wait_send()
    for copy in copies:
        copy.wait()

    nq = gamma_ref.shape[0]
    for q in range(nq):
        name = (me_t * nq + q).astype(f32)

        def kept(tile):
            return jnp.where(tile[2:3, :half] == name, tile[0:2, :half], 0.0)

        total = kept(msg[...])
        if len(peers) <= 16:
            for index in range(len(peers)):
                total = total + kept(inbox[index])
        else:
            total = lax.fori_loop(0, len(peers), lambda i, acc: acc + kept(inbox[i]), total)
        gamma = total[0:1] + bound_ref[q : q + 1, :]
        gamma_ref[q : q + 1, :] = gamma
        dev_ref[q : q + 1, :] = (drive_ref[q : q + 1, :] + total[1:2]) / gamma


def body(
    force_third,
    phase_angle,
    eigenvectors,
    frequencies,
    deviation,
    send_rows,
    trip_table,
    irreducible,
    multiplicity,
    drive_term,
    boundary,
):
    n_clus, n_trip, n_mode = (lax.axis_size(name) for name in ("clus", "trip", "mode"))
    cl, half, flat = force_third.shape
    points, modes, _ = eigenvectors.shape
    slot = send_rows.shape[1] // n_trip
    wide = 512
    rp = up(half, 16)
    ep = up(modes + 1, 16)
    npad = up(flat, wide)
    chunks = npad // wide
    angles = phase_angle.astype(f32)
    trig = jnp.stack([jnp.cos(angles), jnp.sin(angles)], axis=1).astype(bf16).astype(f32)
    tail = jnp.pad(trig, ((0, 0), (0, 6), (0, LANES - trig.shape[2])))
    first = lax.axis_index("mode") == 0
    part = jnp.where(first, eigenvectors[..., :modes], eigenvectors[..., modes:])
    extra = jnp.where(first, frequencies, deviation)[:, None]
    eig = jnp.pad(
        jnp.concatenate([part, extra], axis=1),
        ((0, 0), (0, ep - modes - 1), (0, LANES - modes)),
    )
    n_peers = n_clus * n_trip - 1
    vmem = pl.BlockSpec(memory_space=pltpu.VMEM)
    smem = pl.BlockSpec(memory_space=pltpu.SMEM)
    out = jax.ShapeDtypeStruct(boundary.shape, f32)
    dma = pltpu.SemaphoreType.DMA
    return tuple(
        pl.pallas_call(
            functools.partial(
                kernel, (n_clus, n_trip, n_mode, modes, half, rp, cl, slot, wide)
            ),
            out_shape=(out, out),
            in_specs=[vmem, vmem, vmem, smem, smem, smem, smem, vmem, vmem],
            out_specs=(vmem, vmem),
            scratch_shapes=[
                pltpu.VMEM((n_clus * n_mode * cl * rp, npad), bf16),
                pltpu.VMEM((n_clus, cl, 8, LANES), f32),
                pltpu.VMEM((2 * rp, n_clus * n_mode * cl * rp), bf16),
                pltpu.VMEM((2 * ep, 2 * ep), bf16),
                pltpu.VMEM((8, LANES), f32),
                pltpu.VMEM((n_trip, 8, LANES), f32),
                pltpu.VMEM((n_trip, 3, ep, LANES), bf16),
                pltpu.VMEM((n_trip, 3, ep, LANES), bf16),
                pltpu.VMEM((3, ep, LANES), bf16),
                pltpu.VMEM((3, ep, LANES), bf16),
                pltpu.VMEM((2 * rp, npad), f32),
                pltpu.VMEM((ep * rp, LANES), f32),
                pltpu.VMEM((ep * rp, LANES), f32),
                pltpu.VMEM((rp, LANES), f32),
                pltpu.VMEM((rp * 8, LANES), f32),
                pltpu.VMEM((rp * 8, LANES), f32),
                pltpu.VMEM((8, LANES), f32),
                pltpu.VMEM((n_peers, 8, LANES), f32),
                dma((n_clus, n_mode, chunks)),
                dma((n_clus, n_mode, chunks)),
                dma((n_trip,)),
                dma((n_trip,)),
                dma((n_clus,)),
                dma((n_clus,)),
                dma((n_trip,)),
                dma((n_trip,)),
                dma,
                dma,
                dma((n_peers,)),
                dma((n_peers,)),
            ],
            compiler_params=pltpu.CompilerParams(
                collective_id=0, has_side_effects=True, vmem_limit_bytes=48 * 1024 * 1024
            ),
        )(force_third, tail, eig, send_rows, trip_table, irreducible, multiplicity, drive_term, boundary)
    )


def solution(mesh):
    return jax.shard_map(
        body,
        mesh=mesh,
        in_specs=(
            P("clus", "mode", None),
            P("clus", "trip"),
            P("trip", None, None),
            P("trip", None),
            P("trip", None),
            P("trip", None),
            P("trip", None),
            P("trip"),
            P("trip"),
            P("trip", "mode"),
            P("trip", "mode"),
        ),
        out_specs=(P("trip", "mode"), P("trip", "mode")),
        check_vma=False,
    )
```

```python
import functools

import jax
import jax.numpy as jnp
from jax import lax
from jax.experimental import pallas as pl
from jax.experimental.pallas import tpu as pltpu
from jax.sharding import PartitionSpec as P

smearing = 0.3
MESH = pl.DeviceIdType.MESH
LANES = 128
f32 = jnp.float32
bf16 = jnp.bfloat16


def up(value, step):
    return -(-value // step) * step


def pick(index, options):
    chosen = options[0]
    for position in range(1, len(options)):
        chosen = jnp.where(index == position, options[position], chosen)
    return chosen


def kernel(
    dims,
    force_ref,
    tail_ref,
    eig_ref,
    send_rows_ref,
    table_ref,
    irr_ref,
    mult_ref,
    drive_ref,
    bound_ref,
    gamma_ref,
    dev_ref,
    blocks,
    tails,
    wbuf,
    left,
    asked,
    wanted,
    outgoing,
    arrived,
    mine,
    other,
    zbuf,
    zout,
    zin,
    tre,
    tim,
    w0buf,
    ratebuf,
    coupbuf,
    msg,
    inbox,
    f_send,
    f_recv,
    t_send,
    t_recv,
    c_send,
    c_recv,
    e_send,
    e_recv,
    p_send,
    p_recv,
    m_send,
    m_recv,
):
    n_clus, n_trip, n_mode, modes, half, rp, cl, slot, wide = dims
    ep = eig_ref.shape[1]
    flat = force_ref.shape[2]
    unit_rows = cl * rp
    chunks = zbuf.shape[1] // wide
    me_c = lax.axis_index("clus")
    me_t = lax.axis_index("trip")
    me_m = lax.axis_index("mode")
    sib = (me_c, me_t, 1 - me_m)
    odd = lax.rem(me_t, 2)
    low, high = lax.rem(me_c, 2), me_c // 2
    near = (me_c + (1 - odd) * (1 - 2 * low) + odd * (2 - 4 * high), me_t, me_m)
    far = (me_c + odd * (1 - 2 * low) + (1 - odd) * (2 - 4 * high), me_t, me_m)
    plane = (me_c, me_t + 1 - 2 * odd, me_m)

    peers = []
    for dt in range(n_trip):
        for dc in range(n_clus):
            if dt or dc:
                peers.append((dt, dc))

    def peer_id(dt, dc):
        return (lax.rem(me_c + dc, n_clus), lax.rem(me_t + dt, n_trip), me_m)

    barrier = pltpu.get_barrier_semaphore()
    for dt, dc in peers:
        pl.semaphore_signal(barrier, inc=1, device_id=peer_id(dt, dc), device_id_type=MESH)
    pl.semaphore_signal(barrier, inc=1, device_id=sib, device_id_type=MESH)

    asked[...] = jnp.zeros_like(asked)
    for j in range(3):
        asked[j : j + 1, :] = jnp.full((1, LANES), table_ref[me_c, j].astype(f32))

    whole = half // 16 * 16
    for n in range(chunks):
        lo = n * wide
        hi = min(lo + wide, flat)
        for r in range(cl):
            at = r * rp
            if hi < lo + wide:
                edge = hi // LANES * LANES
                blocks[at : at + rp, edge : lo + wide] = jnp.zeros((rp, lo + wide - edge), bf16)
            blocks[at : at + whole, lo:hi] = force_ref[r, :whole, lo:hi]
            rest = force_ref[r, whole:, lo:hi].astype(f32)
            under = jnp.zeros((rp - half, hi - lo), f32)
            blocks[at + whole : at + rp, lo:hi] = jnp.concatenate([rest, under], axis=0).astype(bf16)

    pl.semaphore_wait(barrier, len(peers) + 1)

    def unit(k, m, n):
        return blocks.at[pl.ds(k * unit_rows, unit_rows), pl.ds(n * wide, wide)]

    started = []

    def copy_of(src, k, m, n, device):
        return pltpu.make_async_remote_copy(
            src_ref=src,
            dst_ref=zin.at[:, pl.ds(n * wide, wide)] if m else unit(k, m, n),
            send_sem=f_send.at[k, m, n],
            recv_sem=f_recv.at[k, m, n],
            device_id=device,
            device_id_type=MESH,
        )

    def send(src, k, m, n, device):
        copy = copy_of(src, k, m, n, device)
        copy.start()
        started.append(copy)

    def got(k, m, n):
        src = zout.at[:, pl.ds(n * wide, wide)] if m else unit(k, m, n)
        copy_of(src, k, m, n, sib).wait_recv()

    asks = []
    for dt in range(1, n_trip):
        copy = pltpu.make_async_remote_copy(
            src_ref=asked,
            dst_ref=wanted.at[dt],
            send_sem=t_send.at[dt],
            recv_sem=t_recv.at[dt],
            device_id=(me_c, lax.rem(me_t + dt, n_trip), me_m),
            device_id_type=MESH,
        )
        copy.start()
        asks.append(copy)
    phase_copies = []
    for k, device in ((1, near), (2, far), (3, (3 - me_c, me_t, me_m))):
        copy = pltpu.make_async_remote_copy(
            src_ref=tail_ref,
            dst_ref=tails.at[k],
            send_sem=c_send.at[k],
            recv_sem=c_recv.at[k],
            device_id=device,
            device_id_type=MESH,
        )
        copy.start()
        phase_copies.append(copy)
    for n in range(chunks):
        send(unit(0, 0, n), 1, 0, n, near)

    def answer(dt, wishes):
        target = lax.rem(me_t - dt + n_trip, n_trip)
        for j in range(3):
            wish = wishes[j : j + 1, :]
            block = jnp.zeros((ep, LANES), f32)
            for k in range(slot):
                row = send_rows_ref[0, target * slot + k]
                name = (me_t * slot + k).astype(f32)
                block = jnp.where(wish == name, eig_ref[row].astype(f32), block)
            outgoing[dt, j] = block.astype(bf16)

    answer(0, asked[...])
    eig_copies = []
    for dt in range(1, n_trip):
        asks[dt - 1].wait()
        answer(dt, wanted[dt])
    for dt in range(1, n_trip):
        copy = pltpu.make_async_remote_copy(
            src_ref=outgoing.at[dt],
            dst_ref=arrived.at[dt],
            send_sem=e_send.at[dt],
            recv_sem=e_recv.at[dt],
            device_id=(me_c, lax.rem(me_t - dt + n_trip, n_trip), me_m),
            device_id_type=MESH,
        )
        copy.start()
        eig_copies.append(copy)
    arrived[0] = outgoing[0]

    def direct(n):
        got(1, 0, n)
        send(unit(1, 0, n), 2, 0, n, plane)
        send(unit(1, 0, n), 3, 0, n, far)

    def second(n):
        got(2, 0, n)
        got(3, 0, n)

    direct(0)
    for copy in eig_copies:
        copy.wait()
    for j in range(3):
        source = table_ref[me_c, j] // slot
        mine[j] = arrived[lax.rem(source - me_t + n_trip, n_trip), j]
    pair = pltpu.make_async_remote_copy(
        src_ref=mine,
        dst_ref=other,
        send_sem=p_send,
        recv_sem=p_recv,
        device_id=sib,
        device_id_type=MESH,
    )
    pair.start()
    direct(1)
    pair.wait()

    first = me_m == 0

    def complex_of(j):
        a = mine[j].astype(f32)
        b = other[j].astype(f32)
        return jnp.where(first, a, b), jnp.where(first, b, a)

    re0, im0 = complex_of(0)
    re1, im1 = complex_of(1)
    re2, im2 = complex_of(2)
    f0 = re0[modes : modes + 1]
    f1, d1 = re1[modes : modes + 1], im1[modes : modes + 1]
    f2, d2 = re2[modes : modes + 1], im2[modes : modes + 1]

    def half_rows(mat, which):
        return pick(which, [mat[m * half : m * half + rp] for m in range(n_mode)])

    fill = jnp.zeros((rp - half, LANES), f32)

    def lead(mat):
        part = pick(me_m, [mat[m * half : (m + 1) * half] for m in range(n_mode)])
        turned = jnp.transpose(jnp.concatenate([part, fill] * cl, axis=0))
        return half_rows(turned, me_m), half_rows(turned, 1 - me_m)

    lead_re = lead(re0)
    lead_im = lead(im0)
    lane_k = lax.broadcasted_iota(jnp.int32, (rp, cl * rp), 1)
    lane = lax.broadcasted_iota(jnp.int32, (1, LANES), 1)

    def weights(k):
        cosines, sines = [], []
        for r in range(cl):
            tail = tail_ref[r] if k == 0 else tails[k, r]
            cosines.append(jnp.sum(jnp.where(lane == me_c, tail[0:1], 0.0), axis=1, keepdims=True))
            sines.append(jnp.sum(jnp.where(lane == me_c, tail[1:2], 0.0), axis=1, keepdims=True))
        cosv, sinv = cosines[0], sines[0]
        for r in range(1, cl):
            cosv = jnp.where(lane_k >= r * rp, cosines[r], cosv)
            sinv = jnp.where(lane_k >= r * rp, sines[r], sinv)
        at = k * unit_rows
        for h in range(2):
            wre, wim = lead_re[h], lead_im[h]
            wbuf[h * 2 * rp : (h + 1) * 2 * rp, at : at + unit_rows] = jnp.concatenate(
                [cosv * wre - sinv * wim, cosv * wim + sinv * wre], axis=0
            ).astype(bf16)

    e2a = jnp.concatenate([re2, im2], axis=1)[:modes].astype(bf16)
    e2b = jnp.concatenate([-im2, re2], axis=1)[:modes].astype(bf16)
    row_id = lax.broadcasted_iota(jnp.int32, (ep, LANES), 0)
    e1re_t = jnp.transpose(jnp.where(row_id < modes, re1, 0.0))[:ep]
    e1im_t = jnp.transpose(jnp.where(row_id < modes, im1, 0.0))[:ep]
    left[:, :ep] = jnp.concatenate([e1re_t, e1im_t], axis=0).astype(bf16)
    left[:, ep:] = jnp.concatenate([-e1im_t, e1re_t], axis=0).astype(bf16)

    def column(row):
        return jnp.transpose(jnp.broadcast_to(row, (LANES, LANES)))

    w0buf[...] = half_rows(column(f0), me_m)
    w1 = jnp.where(row_id < modes, column(f1)[:ep], 1.0)
    w2 = jnp.where(lane < modes, f2, 1.0)
    occ = jnp.where(row_id < modes, column(d1)[:ep], 0.0) + jnp.where(lane < modes, d2, 0.0)
    inverse = 1.0 / (w1 * w2)
    tre[modes * rp :, :] = jnp.zeros(((ep - modes) * rp, LANES), f32)
    tim[modes * rp :, :] = jnp.zeros(((ep - modes) * rp, LANES), f32)

    def share(n):
        cols = slice(n * wide, (n + 1) * wide)
        part = jnp.dot(wbuf[...], blocks[:, cols], preferred_element_type=f32)
        zbuf[:, cols] = part[: 2 * rp]
        zout[:, cols] = part[2 * rp :].astype(bf16)
        send(zout.at[:, pl.ds(n * wide, wide)], 0, 1, n, sib)

    def contract(n):
        got(0, 1, n)
        cols = slice(n * wide, (n + 1) * wide)
        zbuf[:, cols] = zbuf[:, cols] + zin[:, cols].astype(f32)
        for b in range(modes):
            if not n * wide < (b + 1) * modes <= (n + 1) * wide:
                continue
            part = zbuf[:, b * modes : (b + 1) * modes].astype(bf16)
            out = jnp.dot(part[:rp], e2a, preferred_element_type=f32) + jnp.dot(
                part[rp:], e2b, preferred_element_type=f32
            )
            tre[b * rp : (b + 1) * rp, :] = out[:, :LANES]
            tim[b * rp : (b + 1) * rp, :] = out[:, LANES:]

    for copy in phase_copies:
        copy.wait()
    for k in range(4):
        weights(k)

    for n in range(2, chunks + 4):
        if n < chunks:
            direct(n)
        if 0 <= n - 2 < chunks:
            second(n - 2)
        if 0 <= n - 3 < chunks:
            share(n - 3)
        if 0 <= n - 4 < chunks:
            contract(n - 4)

    scaled = 0.5 / (smearing * smearing)
    lower = w1 + w2
    upper = w1 - w2

    def one_pair(s0):
        def rows(ref):
            return jnp.concatenate(
                [ref[pl.ds(s0 + i, ep, stride=rp), :] for i in range(2)], axis=1
            ).astype(bf16)

        both = jnp.concatenate([rows(tre), rows(tim)], axis=0)
        amp = jnp.dot(left[...], both, preferred_element_type=f32)
        square = amp * amp
        square = square[:ep] + square[ep:]
        for i in range(2):
            w0 = w0buf[pl.ds(s0 + i, 1), :]
            decays = w0 - lower
            merges = w0 + upper
            gauss = jnp.exp(-scaled * (decays * decays)) + jnp.exp(-scaled * (merges * merges))
            value = square[:, i * LANES : (i + 1) * LANES] * gauss * inverse
            at = pl.ds(pl.multiple_of((s0 + i) * 8, 8), 8)
            ratebuf[at, :] = jnp.sum(value.reshape(ep // 8, 8, LANES), axis=0)
            coupbuf[at, :] = jnp.sum((value * occ).reshape(ep // 8, 8, LANES), axis=0)

    group = 4

    def modes_step(p, carry):
        for i in range(group):
            one_pair((p * group + i) * 2)
        return carry

    lax.fori_loop(0, rp // (2 * group), modes_step, 0)

    def folded(ref):
        total = ref[pl.ds(0, rp, stride=8), :]
        for i in range(1, 8):
            total = total + ref[pl.ds(i, rp, stride=8), :]
        return jnp.sum(jnp.transpose(total), axis=0, keepdims=True)[:, :half]

    factor = mult_ref[me_c].astype(f32)
    w0_row = pick(me_m, [f0[:, m * half : (m + 1) * half] for m in range(n_mode)])
    rate = folded(ratebuf) / w0_row * factor
    coup = folded(coupbuf) / w0_row * factor
    msg[...] = jnp.zeros_like(msg)
    msg[0:1, 0:half] = rate
    msg[1:2, 0:half] = coup
    msg[2:3, :] = jnp.full((1, LANES), irr_ref[me_c].astype(f32))

    copies = []
    for index, (dt, dc) in enumerate(peers):
        copy = pltpu.make_async_remote_copy(
            src_ref=msg,
            dst_ref=inbox.at[index],
            send_sem=m_send.at[index],
            recv_sem=m_recv.at[index],
            device_id=peer_id(dt, dc),
            device_id_type=MESH,
        )
        copy.start()
        copies.append(copy)
    for copy in started:
        copy.wait_send()
    for copy in copies:
        copy.wait()

    nq = gamma_ref.shape[0]
    for q in range(nq):
        name = (me_t * nq + q).astype(f32)

        def kept(tile):
            return jnp.where(tile[2:3, :half] == name, tile[0:2, :half], 0.0)

        total = kept(msg[...])
        if len(peers) <= 16:
            for index in range(len(peers)):
                total = total + kept(inbox[index])
        else:
            total = lax.fori_loop(0, len(peers), lambda i, acc: acc + kept(inbox[i]), total)
        gamma = total[0:1] + bound_ref[q : q + 1, :]
        gamma_ref[q : q + 1, :] = gamma
        dev_ref[q : q + 1, :] = (drive_ref[q : q + 1, :] + total[1:2]) / gamma


def body(
    force_third,
    phase_angle,
    eigenvectors,
    frequencies,
    deviation,
    send_rows,
    trip_table,
    irreducible,
    multiplicity,
    drive_term,
    boundary,
):
    n_clus, n_trip, n_mode = (lax.axis_size(name) for name in ("clus", "trip", "mode"))
    cl, half, flat = force_third.shape
    points, modes, _ = eigenvectors.shape
    slot = send_rows.shape[1] // n_trip
    wide = 512
    rp = up(half, 16)
    ep = up(modes + 1, 16)
    npad = up(flat, wide)
    chunks = npad // wide
    angles = phase_angle.astype(f32)
    trig = jnp.stack([jnp.cos(angles), jnp.sin(angles)], axis=1).astype(bf16).astype(f32)
    tail = jnp.pad(trig, ((0, 0), (0, 6), (0, LANES - trig.shape[2])))
    first = lax.axis_index("mode") == 0
    part = jnp.where(first, eigenvectors[..., :modes], eigenvectors[..., modes:])
    extra = jnp.where(first, frequencies, deviation)[:, None]
    eig = jnp.pad(
        jnp.concatenate([part, extra], axis=1),
        ((0, 0), (0, ep - modes - 1), (0, LANES - modes)),
    )
    n_peers = n_clus * n_trip - 1
    vmem = pl.BlockSpec(memory_space=pltpu.VMEM)
    smem = pl.BlockSpec(memory_space=pltpu.SMEM)
    out = jax.ShapeDtypeStruct(boundary.shape, f32)
    dma = pltpu.SemaphoreType.DMA
    return tuple(
        pl.pallas_call(
            functools.partial(
                kernel, (n_clus, n_trip, n_mode, modes, half, rp, cl, slot, wide)
            ),
            out_shape=(out, out),
            in_specs=[vmem, vmem, vmem, smem, smem, smem, smem, vmem, vmem],
            out_specs=(vmem, vmem),
            scratch_shapes=[
                pltpu.VMEM((n_clus * cl * rp, npad), bf16),
                pltpu.VMEM((n_clus, cl, 8, LANES), f32),
                pltpu.VMEM((2 * n_mode * rp, n_clus * cl * rp), bf16),
                pltpu.VMEM((2 * ep, 2 * ep), bf16),
                pltpu.VMEM((8, LANES), f32),
                pltpu.VMEM((n_trip, 8, LANES), f32),
                pltpu.VMEM((n_trip, 3, ep, LANES), bf16),
                pltpu.VMEM((n_trip, 3, ep, LANES), bf16),
                pltpu.VMEM((3, ep, LANES), bf16),
                pltpu.VMEM((3, ep, LANES), bf16),
                pltpu.VMEM((2 * rp, npad), f32),
                pltpu.VMEM((2 * rp, npad), bf16),
                pltpu.VMEM((2 * rp, npad), bf16),
                pltpu.VMEM((ep * rp, LANES), f32),
                pltpu.VMEM((ep * rp, LANES), f32),
                pltpu.VMEM((rp, LANES), f32),
                pltpu.VMEM((rp * 8, LANES), f32),
                pltpu.VMEM((rp * 8, LANES), f32),
                pltpu.VMEM((8, LANES), f32),
                pltpu.VMEM((n_peers, 8, LANES), f32),
                dma((n_clus, n_mode, chunks)),
                dma((n_clus, n_mode, chunks)),
                dma((n_trip,)),
                dma((n_trip,)),
                dma((n_clus,)),
                dma((n_clus,)),
                dma((n_trip,)),
                dma((n_trip,)),
                dma,
                dma,
                dma((n_peers,)),
                dma((n_peers,)),
            ],
            compiler_params=pltpu.CompilerParams(
                collective_id=0, has_side_effects=True, vmem_limit_bytes=48 * 1024 * 1024
            ),
        )(force_third, tail, eig, send_rows, trip_table, irreducible, multiplicity, drive_term, boundary)
    )


def solution(mesh):
    return jax.shard_map(
        body,
        mesh=mesh,
        in_specs=(
            P("clus", "mode", None),
            P("clus", "trip"),
            P("trip", None, None),
            P("trip", None),
            P("trip", None),
            P("trip", None),
            P("trip", None),
            P("trip"),
            P("trip"),
            P("trip", "mode"),
            P("trip", "mode"),
        ),
        out_specs=(P("trip", "mode"), P("trip", "mode")),
        check_vma=False,
    )
```
